128 devices in a mesh: tm: 4 (over z_hi, core), mic: 32 (over y, x, z_lo).
Axes of the slice: x: 4, y: 4, z: 4 (z_hi: 2, z_lo: 2; z = z_hi * 2 + z_lo), core: 2. Of those that a mesh axis runs over, the one named last changes fastest.
Arguments:
- samples: bfloat16 [32, 4096, 4096], P('tm', 'mic'), may hold values from -6 to 6
- bin_ids: int32 [16], replicated, may hold values from 1 to 2047
- delays: int32 [4096, 4096], P('mic'), may hold values from 0 to 1023
Outputs:
- source_map: float32 [16, 4096], P('tm', 'mic')
The draws below stay inside these ranges and needn't reach their ends.
All inputs are finite; a program needn't handle non-finite values.
Results may differ from the reference program's by a relative error of at most 0.0013.
Values may be sent and summed in bfloat16 or wider, within the bound.
No kernel may reach another device: no remote copies, remote signals or barrier semaphores. Data moves between devices by JAX's collectives and lax.ppermute only.
A program may use at most 64 MiB of HBM per device.

```python
import math
import jax
import jax.numpy as jnp
from jax import lax

MICS = 4096
L = 4096
F = 16
SEGS = 32
POINTS = 4096


def with_ends(entries, own_key, smallest, largest):
    longest = entries.shape.index(max(entries.shape))
    spots = []
    for shift in (0, 1):
        where = [jax.random.randint(jax.random.fold_in(own_key, axis), (), 0, length) for axis, length in enumerate(entries.shape)]
        where[longest] = (where[longest] + shift) % entries.shape[longest]
        spots.append(tuple(where))
    return entries.at[spots[0]].set(smallest).at[spots[1]].set(largest)


def shard_levels(rng, dims, split, least, top_value):
    def one(position, blocks):
        draws = jax.random.uniform(jax.random.fold_in(jax.random.fold_in(rng, 6), position), (blocks,), jnp.float32, least / len(split), top_value / len(split))
        return jnp.repeat(jnp.exp(draws), dims[position] // blocks).reshape((-1,) + (1,) * (len(dims) - position - 1))

    level = one(*split[0])
    for cut in split[1:]:
        level = level * one(*cut)
    return level


def gaussian(key, dims, scale, limit, split=(), kind=jnp.bfloat16):
    factor_of = shard_levels(key, dims, split, -0.22, 0.18) if split else 1.0
    drawn = jax.random.normal(key, dims, jnp.float32) * scale * factor_of
    return jnp.minimum(jnp.maximum(drawn, -limit), limit).astype(kind)


def setup_inputs(seed: int = 0) -> dict:
    key_list = jax.random.split(jax.random.key(seed), 4)
    samples = gaussian(key_list[0], (SEGS, MICS, L), 1.0, 6.0, ((0, 4), (1, 32)))
    bin_ids = with_ends(jax.random.randint(key_list[1], (F,), 1, L // 2), jax.random.fold_in(key_list[1], 1), 1, (L // 2) - 1).astype(jnp.int32)
    delays = with_ends(jax.random.randint(key_list[2], (POINTS, MICS), 0, 1024), jax.random.fold_in(key_list[2], 1), 0, 1023).astype(jnp.int32)
    return dict(samples=samples, bin_ids=bin_ids, delays=delays)


def dft_table(bin_ids, length):
    sample_index = jnp.arange(length, dtype=jnp.int32)
    window = 0.5 - 0.5 * jnp.cos(2.0 * jnp.pi * sample_index.astype(jnp.float32) / length)
    window_norm = jnp.sqrt(jnp.sum(window * window))
    phase_index = sample_index[:, None] * bin_ids[None, :] % length
    angles = 2.0 * jnp.pi * phase_index.astype(jnp.float32) / length
    cosine = window[:, None] * jnp.cos(angles) / window_norm
    sine_part = -window[:, None] * jnp.sin(angles) / window_norm
    return jnp.stack([cosine, sine_part], axis=-1).reshape(length, -1).astype(jnp.bfloat16)

def reference(samples, bin_ids, delays):
    transform_rows = dft_table(bin_ids, L).astype(jnp.float32)

    def transform(segment):
        result = jnp.dot(segment.astype(jnp.float32), transform_rows, precision=lax.Precision.HIGHEST)
        return result.T.reshape(F, 2, MICS).astype(jnp.bfloat16)
    spectra = lax.map(transform, samples)

    def per_bin(entry):
        bin_value, values = entry
        phases = 2.0 * jnp.pi * (bin_value * delays % L).astype(jnp.float32) / L
        cos_part = jnp.cos(phases).astype(jnp.bfloat16).astype(jnp.float32)
        sin_part = jnp.sin(phases).astype(jnp.bfloat16).astype(jnp.float32)
        flat = values.reshape(SEGS * 2, MICS).astype(jnp.float32)
        along_cos = jnp.dot(flat, cos_part.T, precision=lax.Precision.HIGHEST).reshape(SEGS, 2, POINTS)
        along_sin = jnp.dot(flat, sin_part.T, precision=lax.Precision.HIGHEST).reshape(SEGS, 2, POINTS)
        real_part = (along_cos[:, 0] - along_sin[:, 1]) / math.sqrt(MICS)
        imag_part = (along_cos[:, 1] + along_sin[:, 0]) / math.sqrt(MICS)
        return lax.optimization_barrier(jnp.sum(real_part * real_part + imag_part * imag_part, axis=0)) / SEGS
    return lax.map(per_bin, (bin_ids, jnp.moveaxis(spectra, 1, 0)))
```

```python
import math

import jax
import jax.numpy as jnp
from jax import lax
from jax.experimental import pallas as pl
from jax.experimental.pallas import tpu as pltpu
from jax.sharding import PartitionSpec as P

AXES = ("tm", "mic")
SHIFTS = (1, 3, 2)
OFFSETS = (0, 1, 3, 2)
ROUND = 12582912.0
SIN_POLY = (4.442882919124343, -7.30824568650904, 3.6063542184324877, -0.8461116503718901, 0.10982451642219883)
COS_POLY = (1.414213496255228, -6.978850948563807, 5.73946037690717, -1.8835579059870113, 0.31068802752761115)


def horner(coefs, z):
    value = coefs[-1]
    for coef in coefs[-2::-1]:
        value = value * z + coef
    return value


def cos_sin(turns):
    r = turns - ((turns + ROUND) - ROUND)
    z = r * r
    s = horner(SIN_POLY, z) * r
    c = horner(COS_POLY, z)
    return 1.0 - s * s, s * c


def transform_kernel(place, bins, seg, keep, send, table, sums, blocks):
    step = pl.program_id(0)
    n_bins = bins.shape[0]
    length = seg.shape[2]
    n_segs = sums.shape[0]
    chunk = 512

    @pl.when(step == 0)
    def _():
        scale = bins[:, 0:1]
        for k in range(length // chunk):
            n = (lax.broadcasted_iota(jnp.int32, (n_bins, chunk), 1) + k * chunk).astype(jnp.float32)
            hann = 0.5 - 0.5 * cos_sin(n * (1.0 / length))[0]
            weight = hann * (1.0 / math.sqrt(0.375 * length))
            cos, sin = cos_sin(n * scale)
            table[0:n_bins, k * chunk : (k + 1) * chunk] = (weight * cos).astype(jnp.bfloat16)
            table[n_bins:, k * chunk : (k + 1) * chunk] = (-weight * sin).astype(jnp.bfloat16)

    sums[step] = lax.dot_general(
        table[...], seg[0], (((1,), (1,)), ((), ())), preferred_element_type=jnp.float32
    )

    @pl.when(step == n_segs - 1)
    def _():
        for b in range(n_bins):
            rows = jnp.concatenate([sums[:, b, :], sums[:, n_bins + b, :]], axis=0)
            blocks[b // 4, (b % 4) * 16 : (b % 4 + 1) * 16, :] = rows.astype(jnp.bfloat16)
        zh = place[0]
        core = place[1]
        keep[0] = blocks[zh * 2 + core]
        keep[1] = blocks[(1 - zh) * 2 + core]
        send[0] = blocks[zh * 2 + 1 - core]
        send[1] = blocks[(1 - zh) * 2 + 1 - core]


def transform(place, bins, samples):
    segs, mics, length = samples.shape
    n_bins = bins.shape[0]
    block = jax.ShapeDtypeStruct((2, n_bins // 4 * 2 * segs, mics), jnp.bfloat16)
    return pl.pallas_call(
        transform_kernel,
        grid_spec=pltpu.PrefetchScalarGridSpec(
            num_scalar_prefetch=1,
            grid=(segs,),
            in_specs=[
                pl.BlockSpec((n_bins, 128), lambda i, place: (0, 0)),
                pl.BlockSpec((1, mics, length), lambda i, place: (i, 0, 0)),
            ],
            out_specs=[pl.BlockSpec(block.shape, lambda i, place: (0, 0, 0))] * 2,
            scratch_shapes=[
                pltpu.VMEM((2 * n_bins, length), jnp.bfloat16),
                pltpu.VMEM((segs, 2 * n_bins, mics), jnp.float32),
                pltpu.VMEM((4,) + block.shape[1:], jnp.bfloat16),
            ],
        ),
        out_shape=[block, block],
        name="transform",
    )(place, bins, samples)


def narrow_kernel(place, delays, out):
    other = 1 - place[2]
    for j in range(out.shape[0]):
        first = delays[:, j * 256 : j * 256 + 128]
        second = delays[:, j * 256 + 128 : (j + 1) * 256]
        out[j] = jnp.where(other == 0, first, second).astype(jnp.int16)


def narrow(place, delays):
    points, mics = delays.shape
    return pl.pallas_call(
        narrow_kernel,
        grid_spec=pltpu.PrefetchScalarGridSpec(
            num_scalar_prefetch=1,
            grid=(4,),
            in_specs=[pl.BlockSpec((points, mics // 4), lambda i, place: (0, i))],
            out_specs=pl.BlockSpec((mics // 1024, points, 128), lambda i, place: (i, 0, 0)),
        ),
        out_shape=jax.ShapeDtypeStruct((mics // 256, points, 128), jnp.int16),
        name="narrow",
    )(place, delays)


def block_of(index, place):
    second = index // 4
    first = index % 4
    second = second ^ (second >> 1)
    first = first ^ (first >> 1)
    dx = first + place[1] * (second - first)
    dy = second + place[1] * (first - second)
    return ((place[3] - dy) & 3) * 4 + ((place[4] - dx) & 3)


def steer_kernel(place, bins, first, second, out):
    n_bins, rows, _ = out.shape[1:]
    points = rows // 2
    for half, delays in enumerate((first, second)):
        for k in range(points // 32):
            if len(delays.shape) == 3:
                d = delays[0, k * 32 : (k + 1) * 32, :].astype(jnp.int32)
            else:
                d = delays[k * 32 : (k + 1) * 32, :]
            d = d.astype(jnp.float32)
            for f in range(n_bins):
                cos, sin = cos_sin(d * bins[f])
                lanes = slice(half * 128, (half + 1) * 128)
                out[0, f, k * 32 : (k + 1) * 32, lanes] = cos.astype(jnp.bfloat16)
                out[0, f, points + k * 32 : points + (k + 1) * 32, lanes] = sin.astype(jnp.bfloat16)


def steer_tables(place, bins, delays, own):
    points = 128
    n_bins = bins.shape[0]
    pairs = 8
    if own:
        specs = [
            pl.BlockSpec((points, 128), lambda i, place, h=h: (0, block_of(2 * i + h, place) * 2 + place[2]))
            for h in range(2)
        ]
    else:
        specs = [
            pl.BlockSpec((1, points, 128), lambda i, place, h=h: (block_of(2 * i + h, place), 0, 0))
            for h in range(2)
        ]
    return pl.pallas_call(
        steer_kernel,
        grid_spec=pltpu.PrefetchScalarGridSpec(
            num_scalar_prefetch=1,
            grid=(pairs,),
            in_specs=[pl.BlockSpec(memory_space=pltpu.SMEM)] + specs,
            out_specs=pl.BlockSpec((1, n_bins, 2 * points, 256), lambda i, place: (i, 0, 0, 0)),
        ),
        out_shape=jax.ShapeDtypeStruct((pairs, n_bins, 2 * points, 256), jnp.bfloat16),
        name="steer_own" if own else "steer_partner",
    )(place, bins, delays, delays)


def apply_kernel(first, last, *refs):
    if first:
        spectra, own, partner, own_out, partner_out = refs
    else:
        spectra, own, partner, own_in, partner_in, own_out, partner_out = refs
    f = pl.program_id(0)
    start = pl.multiple_of(f * 16, 16)
    sums = [None, None]
    for pair in range(2):
        left = jnp.concatenate(
            [
                jnp.concatenate(
                    [spectra[2 * pair + h, src, pl.ds(start, 16), :] for src in range(4)], axis=0
                )
                for h in range(2)
            ],
            axis=1,
        )
        for which, table in enumerate((own, partner)):
            product = lax.dot_general(
                left, table[pair, 0], (((1,), (1,)), ((), ())), preferred_element_type=jnp.float32
            )
            sums[which] = product if sums[which] is None else sums[which] + product
    if not first:
        sums[0] = sums[0] + own_in[0]
        sums[1] = sums[1] + partner_in[0]
    for total, out in zip(sums, (own_out, partner_out)):
        if last:
            real, imag = [], []
            for src in range(4):
                re_rows = total[src * 16 : src * 16 + 8]
                im_rows = total[src * 16 + 8 : src * 16 + 16]
                real.append(re_rows[:, :128] - im_rows[:, 128:])
                imag.append(im_rows[:, :128] + re_rows[:, 128:])
            out[0] = jnp.concatenate(real + imag, axis=0)
        else:
            out[0] = total


def apply_tables(spectra, own, partner, index, sums, last):
    n_bins = own.shape[1]
    wide = pl.BlockSpec((2, 1, 256, 256), lambda f: (index, f, 0, 0))
    part = pl.BlockSpec((1, 64, 256), lambda f: (f, 0, 0))
    shape = (n_bins, 64, 128) if last else (n_bins, 64, 256)
    return pl.pallas_call(
        lambda *refs: apply_kernel(sums is None, last, *refs),
        grid=(n_bins,),
        in_specs=[pl.BlockSpec(spectra.shape, lambda f: (0, 0, 0, 0)), wide, wide]
        + ([] if sums is None else [part, part]),
        out_specs=[pl.BlockSpec((1,) + shape[1:], lambda f: (f, 0, 0))] * 2,
        out_shape=[jax.ShapeDtypeStruct(shape, jnp.float32)] * 2,
        name="apply",
    )(spectra, own, partner, *(sums or ()))


def route(move):
    pairs = []
    for tm in range(4):
        for mic in range(32):
            zh, core, y, x, zl = tm // 2, tm % 2, mic // 8, mic // 2 % 4, mic % 2
            zh, core, y, x, zl = move(zh, core, y, x, zl)
            pairs.append((tm * 32 + mic, (zh * 2 + core) * 32 + y % 4 * 8 + x % 4 * 2 + zl))
    return pairs


def send(value, move):
    return lax.ppermute(value, AXES, route(move))


def per_device(samples, bin_ids, delays):
    tm = lax.axis_index("tm")
    mic = lax.axis_index("mic")
    length = samples.shape[2]
    place = jnp.stack([tm >> 1, tm & 1, mic & 1, mic >> 3, (mic >> 1) & 3]).astype(jnp.int32)
    turns = bin_ids.astype(jnp.float32) / length
    own_turns = lax.dynamic_slice_in_dim(turns, tm * 4, 4)

    narrowed = narrow(place, delays)
    partner_delays = send(narrowed, lambda zh, c, y, x, zl: (zh, c, y, x, 1 - zl))

    keep, give = transform(place, jnp.broadcast_to(turns[:, None], (turns.shape[0], 128)), samples)
    got = send(give, lambda zh, c, y, x, zl: (zh, 1 - c, y, x, zl))
    far = send(
        jnp.concatenate([keep[1:], got[1:]]), lambda zh, c, y, x, zl: (1 - zh, c, y, x, zl)
    )
    column = jnp.concatenate([keep[:1], got[:1], far])

    own = steer_tables(place, own_turns, delays, True)
    partner = steer_tables(place, own_turns, partner_delays, False)

    line = [column]
    for d in SHIFTS:
        line.append(
            send(
                column,
                lambda zh, c, y, x, zl: (zh, c, y + d, x, zl) if c else (zh, c, y, x + d, zl),
            )
        )
    line = jnp.stack(line)
    planes = [line]
    for d in SHIFTS:
        planes.append(
            send(
                line,
                lambda zh, c, y, x, zl: (zh, c, y, x + d, zl) if c else (zh, c, y + d, x, zl),
            )
        )
    sums = None
    for i, plane in enumerate(planes):
        sums = apply_tables(plane, own, partner, i, sums, i == 3)
    mine, theirs = sums
    theirs = send(theirs, lambda zh, c, y, x, zl: (zh, c, y, x, 1 - zl))
    total = mine + theirs
    seg_count = samples.shape[0] * lax.axis_size("tm")
    return jnp.sum(total * total, axis=1) / (delays.shape[1] * seg_count)


def solution(mesh):
    placed = (P("tm", "mic", None), P(), P("mic", None))
    return jax.shard_map(
        per_device, mesh=mesh, in_specs=placed, out_specs=P("tm", "mic"), check_vma=False
    )
```

```python
import math

import jax
import jax.numpy as jnp
from jax import lax
from jax.experimental import pallas as pl
from jax.experimental.pallas import tpu as pltpu
from jax.sharding import PartitionSpec as P


AXES = ("tm", "mic")
SHIFTS = (2, 1, 3)
ROUND = 12582912.0
GROUPS = (3, 3, 2)
OWN = (2, 4, 2)
SIN_POLY = (4.442882919124343, -7.30824568650904, 3.6063542184324877, -0.8461116503718901, 0.10982451642219883)
COS_POLY = (1.414213496255228, -6.978850948563807, 5.73946037690717, -1.8835579059870113, 0.31068802752761115)


def horner(coefs, z):
    value = coefs[-1]
    for coef in coefs[-2::-1]:
        value = value * z + coef
    return value


def cos_sin(turns):
    r = turns - ((turns + ROUND) - ROUND)
    z = r * r
    s = horner(SIN_POLY, z) * r
    c = horner(COS_POLY, z)
    return 1.0 - s * s, s * c


VMEM = pl.BlockSpec(memory_space=pltpu.VMEM)
SMEM = pl.BlockSpec(memory_space=pltpu.SMEM)
PARAMS = pltpu.CompilerParams(vmem_limit_bytes=16 * 2**20)
WIDE = pltpu.CompilerParams(vmem_limit_bytes=58 * 2**20)


def position():
    tm = lax.axis_index("tm")
    mic = lax.axis_index("mic")
    return tm >> 1, tm & 1, mic >> 3, (mic >> 1) & 3, mic & 1


def transform_kernel(
    bins_in, delays_in, samples, keep, send, mine, half, bins, delays, segs, sems, table, sums, blocks
):
    zh, core, _, _, zl = position()
    n_segs, mics, length = segs.shape
    n_bins = bins.shape[0]
    chunk = 512
    copies = [
        pltpu.make_async_copy(samples.at[s], segs.at[s], sems.at[s]) for s in range(n_segs)
    ]
    bins_copy = pltpu.make_async_copy(bins_in, bins, sems.at[n_segs])
    delays_copy = pltpu.make_async_copy(delays_in, delays, sems.at[n_segs + 1])
    bins_copy.start()
    for s in range(GROUPS[0]):
        copies[s].start()

    bins_copy.wait()
    row = lax.broadcasted_iota(jnp.int32, (n_bins, chunk), 0)
    scale = jnp.zeros((n_bins, chunk), jnp.float32)
    for b in range(n_bins):
        scale = jnp.where(row == b, bins[b].astype(jnp.float32) * (1.0 / length), scale)
    lane = lax.broadcasted_iota(jnp.int32, (n_bins, chunk), 1)
    for k in range(length // chunk):
        n = (lane + k * chunk).astype(jnp.float32)
        hann = 0.5 - 0.5 * cos_sin(n[0:8] * (1.0 / length))[0]
        weight = jnp.concatenate([hann, hann], axis=0) * (1.0 / math.sqrt(0.375 * length))
        cos, sin = cos_sin(n * scale)
        table[0:n_bins, k * chunk : (k + 1) * chunk] = (weight * cos).astype(jnp.bfloat16)
        table[n_bins:, k * chunk : (k + 1) * chunk] = (-weight * sin).astype(jnp.bfloat16)

    done = 0
    for g, group in enumerate(GROUPS):
        for s in range(done, done + group):
            copies[s].wait()
            if s + GROUPS[0] < n_segs:
                copies[s + GROUPS[0]].start()
        if g == 0:
            delays_copy.start()
        if g == len(GROUPS) - 1:
            delays_copy.wait()
        product = lax.dot_general(
            segs[done : done + group].reshape(group * mics, length),
            table[...],
            (((1,), (1,)), ((), ())),
            preferred_element_type=jnp.float32,
        )
        for s in range(group):
            sums[done + s] = product[s * mics : (s + 1) * mics].T
        done += group

    for j in range(mine.shape[0]):
        first = delays[:, j * 256 : j * 256 + 128]
        second = delays[:, j * 256 + 128 : (j + 1) * 256]
        mine[j] = jnp.where(zl == 0, first, second).astype(jnp.int16)
        other = jnp.where(zl == 0, second, first).astype(jnp.int16)

        @pl.when(j // half.shape[0] == core)
        def _():
            half[j % half.shape[0]] = other

    for b in range(n_bins):
        rows = jnp.concatenate([sums[:, b, :], sums[:, n_bins + b, :]], axis=0)
        blocks[b // 4, (b % 4) * 16 : (b % 4 + 1) * 16, :] = rows.astype(jnp.bfloat16)
    keep[0] = blocks[zh * 2 + core]
    keep[1] = blocks[(1 - zh) * 2 + core]
    send[0] = blocks[zh * 2 + 1 - core]
    send[1] = blocks[(1 - zh) * 2 + 1 - core]


def transform(bins, delays, samples):
    segs, mics, length = samples.shape
    points = delays.shape[0]
    n_bins = bins.shape[0]
    block = (2, n_bins // 4 * 2 * segs, mics)
    blocks = delays.shape[1] // 256
    return pl.pallas_call(
        transform_kernel,
        in_specs=[pl.BlockSpec(memory_space=pltpu.HBM)] * 3,
        out_specs=[VMEM] * 4,
        out_shape=[
            pltpu.VMEM(block, jnp.bfloat16),
            pltpu.VMEM(block, jnp.bfloat16),
            pltpu.VMEM((blocks, points, 128), jnp.int16),
            pltpu.VMEM((blocks // 2, points, 128), jnp.int16),
        ],
        scratch_shapes=[
            pltpu.SMEM((n_bins,), jnp.int32),
            pltpu.VMEM(delays.shape, delays.dtype),
            pltpu.VMEM((segs, mics, length), jnp.bfloat16),
            pltpu.SemaphoreType.DMA((segs + 2,)),
            pltpu.VMEM((2 * n_bins, length), jnp.bfloat16),
            pltpu.VMEM((segs, 2 * n_bins, mics), jnp.float32),
            pltpu.VMEM((4,) + block[1:], jnp.bfloat16),
        ],
        compiler_params=WIDE,
        name="transform",
    )(bins, delays, samples)


def arrival(index):
    return ((index & 1) << 1) | (index >> 1)


def block_of(index):
    _, core, y, x, _ = position()
    second = arrival(index >> 2)
    first = arrival(index & 3)
    dx = first + core * (second - first)
    dy = second + core * (first - second)
    return ((y - dy) & 3) * 4 + ((x - dx) & 3)


def steer_kernel(start, halves, bins, *refs):
    out = refs[-1]
    pairs, n_bins, points, _ = out.shape
    tm = lax.axis_index("tm")
    core = tm & 1
    turns = [bins[tm * n_bins + f].astype(jnp.float32) * (1.0 / 4096) for f in range(n_bins)]

    def body(pair, carry):
        for half in range(2):
            block = block_of((start + pair) * 2 + half)
            for k in range(points // 32):
                rows = slice(k * 32, (k + 1) * 32)
                if halves:
                    kept = (block >> 3) == core
                    d = jnp.where(kept, refs[0][block & 7, rows, :], refs[1][block & 7, rows, :])
                else:
                    d = refs[0][block, rows, :]
                d = d.astype(jnp.int32).astype(jnp.float32)
                for f in range(n_bins):
                    cos, sin = cos_sin(d * turns[f])
                    out[pair, f, rows, half * 128 : (half + 1) * 128] = cos.astype(jnp.bfloat16)
                    out[pair, f, rows, 256 + half * 128 : 384 + half * 128] = sin.astype(jnp.bfloat16)
        return carry

    lax.fori_loop(0, pairs, body, 0)


def steer_tables(bins, delays, start, pairs):
    return pl.pallas_call(
        lambda *refs: steer_kernel(start, len(delays) == 2, *refs),
        in_specs=[SMEM] + [VMEM] * len(delays),
        out_specs=VMEM,
        out_shape=pltpu.VMEM((pairs, bins.shape[0] // 4, 128, 512), jnp.bfloat16),
        compiler_params=PARAMS,
        name="steer",
    )(bins, *delays)


def apply_kernel(n_planes, n_tables, start, carried, last, *refs):
    planes = refs[:n_planes]
    tables = refs[n_planes : n_planes + n_tables]
    before = refs[n_planes + n_tables] if carried else None
    out = refs[-1]
    pairs = [(table, p) for table in tables for p in range(table.shape[0])]
    n_bins = tables[0].shape[1]
    for f in range(n_bins):
        total = before[f] if carried else None
        for i, plane in enumerate(planes):
            for q in range(2):
                cos_cols, sin_cols = [], []
                for h in range(2):
                    both = [
                        plane[2 * q + h, src, f * 16 : (f + 1) * 16, :].astype(jnp.float32)
                        for src in range(4)
                    ]
                    real = [b[0:8] for b in both]
                    imag = [b[8:16] for b in both]
                    cos_cols.append(jnp.concatenate(real + imag, axis=0))
                    sin_cols.append(jnp.concatenate([-v for v in imag] + real, axis=0))
                columns = jnp.concatenate(cos_cols + sin_cols, axis=1).astype(jnp.bfloat16)
                table, p = pairs[start + 2 * i + q]
                product = lax.dot_general(
                    table[p, f],
                    columns,
                    (((1,), (1,)), ((), ())),
                    preferred_element_type=jnp.float32,
                )
                total = product if total is None else total + product
        if last:
            out[f // 2, :, (f % 2) * 64 : (f % 2 + 1) * 64] = total.astype(out.dtype)
        else:
            out[f] = total


def apply_tables(planes, tables, start, before, kind):
    n_bins = tables[0].shape[1]
    shape = (n_bins, 128, 64) if kind is None else (n_bins // 2, 128, 128)
    args = (*planes, *tables) + (() if before is None else (before,))
    return pl.pallas_call(
        lambda *refs: apply_kernel(
            len(planes), len(tables), start, before is not None, kind is not None, *refs
        ),
        in_specs=[VMEM] * len(args),
        out_specs=VMEM,
        out_shape=pltpu.VMEM(shape, kind or jnp.float32),
        compiler_params=PARAMS,
        name="apply",
    )(*args)


def power_kernel(scale, mine, theirs, out):
    for k in range(mine.shape[0]):
        total = mine[k] + theirs[k].astype(jnp.float32)
        squares = (total * total).T
        for f in range(2):
            power = jnp.sum(squares[f * 64 : (f + 1) * 64], axis=0, keepdims=True)
            out[2 * k + f : 2 * k + f + 1, :] = power * scale


def powers(mine, theirs, scale):
    return pl.pallas_call(
        lambda *refs: power_kernel(scale, *refs),
        in_specs=[VMEM] * 2,
        out_specs=VMEM,
        out_shape=jax.ShapeDtypeStruct((2 * mine.shape[0], mine.shape[1]), jnp.float32),
        compiler_params=PARAMS,
        name="powers",
    )(mine, theirs)


def route(move):
    pairs = []
    for tm in range(4):
        for mic in range(32):
            zh, core, y, x, zl = tm // 2, tm % 2, mic // 8, mic // 2 % 4, mic % 2
            zh, core, y, x, zl = move(zh, core, y, x, zl)
            pairs.append((tm * 32 + mic, (zh * 2 + core) * 32 + y % 4 * 8 + x % 4 * 2 + zl))
    return pairs


def send(value, move):
    return lax.ppermute(value, AXES, route(move))


def per_device(samples, bin_ids, delays):
    keep, give, own_delays, half = transform(bin_ids, delays, samples)
    got = send(give, lambda zh, c, y, x, zl: (zh, 1 - c, y, x, zl))
    half = send(half, lambda zh, c, y, x, zl: (zh, c, y, x, 1 - zl))
    partner_delays = half, send(half, lambda zh, c, y, x, zl: (zh, 1 - c, y, x, zl))
    away = jnp.concatenate([keep[1:], got[1:]])
    far = send(away, lambda zh, c, y, x, zl: (1 - zh, c, y, x, zl))
    column = jnp.concatenate([keep[:1], got[:1], far])

    own, start = [], 0
    for pairs in OWN:
        own.append(steer_tables(bin_ids, (own_delays,), start, pairs))
        start += pairs
    partner = steer_tables(bin_ids, partner_delays, 0, 8)

    def first(d):
        return lambda zh, c, y, x, zl: (zh, c, y + d, x, zl) if c else (zh, c, y, x + d, zl)

    def second(d):
        return lambda zh, c, y, x, zl: (zh, c, y, x + d, zl) if c else (zh, c, y + d, x, zl)

    line = [column]
    for d in SHIFTS:
        line.append(send(column, first(d)))
    line = jnp.stack(line)
    planes = [line]
    for d in SHIFTS:
        planes.append(send(line, second(d)))
    theirs = apply_tables(planes[:1], (partner,), 0, None, None)
    theirs = apply_tables(planes[1:3], (partner,), 2, theirs, None)
    theirs = apply_tables(planes[3:], (partner,), 6, theirs, jnp.bfloat16)
    theirs = send(theirs, lambda zh, c, y, x, zl: (zh, c, y, x, 1 - zl))
    mine = apply_tables(planes, own, 0, None, jnp.float32)
    seg_count = samples.shape[0] * lax.axis_size("tm")
    return powers(mine, theirs, 1.0 / (delays.shape[1] * seg_count))


def solution(mesh):
    placed = (P("tm", "mic", None), P(), P("mic", None))
    return jax.shard_map(
        per_device, mesh=mesh, in_specs=placed, out_specs=P("tm", "mic"), check_vma=False
    )
```

```python
import math

import jax
import jax.numpy as jnp
from jax import lax
from jax.experimental import pallas as pl
from jax.experimental.pallas import tpu as pltpu
from jax.sharding import PartitionSpec as P


AXES = ("tm", "mic")
SHIFTS = (2, 1, 3)
ROUND = 12582912.0
GROUPS = (3, 3, 2)
OWN = (2, 4, 2)
SIN_POLY = (4.442882919124343, -7.30824568650904, 3.6063542184324877, -0.8461116503718901, 0.10982451642219883)
COS_POLY = (1.414213496255228, -6.978850948563807, 5.73946037690717, -1.8835579059870113, 0.31068802752761115)


def horner(coefs, z):
    value = coefs[-1]
    for coef in coefs[-2::-1]:
        value = value * z + coef
    return value


def cos_sin(turns):
    r = turns - ((turns + ROUND) - ROUND)
    z = r * r
    s = horner(SIN_POLY, z) * r
    c = horner(COS_POLY, z)
    return 1.0 - s * s, s * c


VMEM = pl.BlockSpec(memory_space=pltpu.VMEM)
SMEM = pl.BlockSpec(memory_space=pltpu.SMEM)
PARAMS = pltpu.CompilerParams(vmem_limit_bytes=16 * 2**20)
WIDE = pltpu.CompilerParams(vmem_limit_bytes=58 * 2**20)


def position():
    tm = lax.axis_index("tm")
    mic = lax.axis_index("mic")
    return tm >> 1, tm & 1, mic >> 3, (mic >> 1) & 3, mic & 1


def transform_kernel(
    bins_in, delays_in, samples, keep, send, mine, half, bins, delays, segs, sems, table, sums, blocks
):
    zh, core, _, _, zl = position()
    n_segs, mics, length = segs.shape
    n_bins = bins.shape[0]
    chunk = 512
    copies = [
        pltpu.make_async_copy(samples.at[s], segs.at[s], sems.at[s]) for s in range(n_segs)
    ]
    bins_copy = pltpu.make_async_copy(bins_in, bins, sems.at[n_segs])
    delays_copy = pltpu.make_async_copy(delays_in, delays, sems.at[n_segs + 1])
    bins_copy.start()
    for s in range(GROUPS[0]):
        copies[s].start()

    bins_copy.wait()
    row = lax.broadcasted_iota(jnp.int32, (n_bins, chunk), 0)
    scale = jnp.zeros((n_bins, chunk), jnp.float32)
    for b in range(n_bins):
        scale = jnp.where(row == b, bins[b].astype(jnp.float32) * (1.0 / length), scale)
    lane = lax.broadcasted_iota(jnp.int32, (n_bins, chunk), 1)
    for k in range(length // chunk):
        n = (lane + k * chunk).astype(jnp.float32)
        hann = 0.5 - 0.5 * cos_sin(n[0:8] * (1.0 / length))[0]
        weight = jnp.concatenate([hann, hann], axis=0) * (1.0 / math.sqrt(0.375 * length))
        cos, sin = cos_sin(n * scale)
        table[0:n_bins, k * chunk : (k + 1) * chunk] = (weight * cos).astype(jnp.bfloat16)
        table[n_bins:, k * chunk : (k + 1) * chunk] = (-weight * sin).astype(jnp.bfloat16)

    done = 0
    for g, group in enumerate(GROUPS):
        for s in range(done, done + group):
            copies[s].wait()
            if s + GROUPS[0] < n_segs:
                copies[s + GROUPS[0]].start()
        if g == 0:
            delays_copy.start()
        if g == len(GROUPS) - 1:
            delays_copy.wait()
        product = lax.dot_general(
            segs[done : done + group].reshape(group * mics, length),
            table[...],
            (((1,), (1,)), ((), ())),
            preferred_element_type=jnp.float32,
        )
        for s in range(group):
            sums[done + s] = product[s * mics : (s + 1) * mics].T
        done += group

    for j in range(mine.shape[0]):
        first = delays[:, j * 256 : j * 256 + 128]
        second = delays[:, j * 256 + 128 : (j + 1) * 256]
        mine[j] = jnp.where(zl == 0, first, second).astype(jnp.int16)
        other = jnp.where(zl == 0, second, first).astype(jnp.int16)

        half[j] = other

    for b in range(n_bins):
        rows = jnp.concatenate([sums[:, b, :], sums[:, n_bins + b, :]], axis=0)
        blocks[b // 4, (b % 4) * 16 : (b % 4 + 1) * 16, :] = rows.astype(jnp.bfloat16)
    keep[0] = blocks[zh * 2 + core]
    keep[1] = blocks[(1 - zh) * 2 + core]
    send[0] = blocks[zh * 2 + 1 - core]
    send[1] = blocks[(1 - zh) * 2 + 1 - core]


def transform(bins, delays, samples):
    segs, mics, length = samples.shape
    points = delays.shape[0]
    n_bins = bins.shape[0]
    block = (2, n_bins // 4 * 2 * segs, mics)
    blocks = delays.shape[1] // 256
    return pl.pallas_call(
        transform_kernel,
        in_specs=[pl.BlockSpec(memory_space=pltpu.HBM)] * 3,
        out_specs=[VMEM] * 4,
        out_shape=[
            pltpu.VMEM(block, jnp.bfloat16),
            pltpu.VMEM(block, jnp.bfloat16),
            pltpu.VMEM((blocks, points, 128), jnp.int16),
            pltpu.VMEM((blocks, points, 128), jnp.int16),
        ],
        scratch_shapes=[
            pltpu.SMEM((n_bins,), jnp.int32),
            pltpu.VMEM(delays.shape, delays.dtype),
            pltpu.VMEM((segs, mics, length), jnp.bfloat16),
            pltpu.SemaphoreType.DMA((segs + 2,)),
            pltpu.VMEM((2 * n_bins, length), jnp.bfloat16),
            pltpu.VMEM((segs, 2 * n_bins, mics), jnp.float32),
            pltpu.VMEM((4,) + block[1:], jnp.bfloat16),
        ],
        compiler_params=WIDE,
        name="transform",
    )(bins, delays, samples)


def arrival(index):
    return ((index & 1) << 1) | (index >> 1)


def block_of(index):
    _, core, y, x, _ = position()
    second = arrival(index >> 2)
    first = arrival(index & 3)
    dx = first + core * (second - first)
    dy = second + core * (first - second)
    return ((y - dy) & 3) * 4 + ((x - dx) & 3)


def steer_kernel(start, halves, bins, *refs):
    out = refs[-1]
    pairs, n_bins, points, _ = out.shape
    tm = lax.axis_index("tm")
    core = tm & 1
    turns = [bins[tm * n_bins + f].astype(jnp.float32) * (1.0 / 4096) for f in range(n_bins)]

    def body(pair, carry):
        for half in range(2):
            block = block_of((start + pair) * 2 + half)
            for k in range(points // 32):
                rows = slice(k * 32, (k + 1) * 32)
                if halves:
                    kept = (block >> 3) == core
                    d = jnp.where(kept, refs[0][block & 7, rows, :], refs[1][block & 7, rows, :])
                else:
                    d = refs[0][block, rows, :]
                d = d.astype(jnp.int32).astype(jnp.float32)
                for f in range(n_bins):
                    cos, sin = cos_sin(d * turns[f])
                    out[pair, f, rows, half * 128 : (half + 1) * 128] = cos.astype(jnp.bfloat16)
                    out[pair, f, rows, 256 + half * 128 : 384 + half * 128] = sin.astype(jnp.bfloat16)
        return carry

    lax.fori_loop(0, pairs, body, 0)


def steer_tables(bins, delays, start, pairs):
    return pl.pallas_call(
        lambda *refs: steer_kernel(start, len(delays) == 2, *refs),
        in_specs=[SMEM] + [VMEM] * len(delays),
        out_specs=VMEM,
        out_shape=pltpu.VMEM((pairs, bins.shape[0] // 4, 128, 512), jnp.bfloat16),
        compiler_params=PARAMS,
        name="steer",
    )(bins, *delays)


def apply_kernel(n_planes, n_tables, start, carried, last, *refs):
    planes = refs[:n_planes]
    tables = refs[n_planes : n_planes + n_tables]
    before = refs[n_planes + n_tables] if carried else None
    out = refs[-1]
    pairs = [(table, p) for table in tables for p in range(table.shape[0])]
    n_bins = tables[0].shape[1]
    for f in range(n_bins):
        total = before[f] if carried else None
        for i, plane in enumerate(planes):
            for q in range(2):
                cos_cols, sin_cols = [], []
                for h in range(2):
                    both = [
                        plane[2 * q + h, src, f * 16 : (f + 1) * 16, :].astype(jnp.float32)
                        for src in range(4)
                    ]
                    real = [b[0:8] for b in both]
                    imag = [b[8:16] for b in both]
                    cos_cols.append(jnp.concatenate(real + imag, axis=0))
                    sin_cols.append(jnp.concatenate([-v for v in imag] + real, axis=0))
                columns = jnp.concatenate(cos_cols + sin_cols, axis=1).astype(jnp.bfloat16)
                table, p = pairs[start + 2 * i + q]
                product = lax.dot_general(
                    table[p, f],
                    columns,
                    (((1,), (1,)), ((), ())),
                    preferred_element_type=jnp.float32,
                )
                total = product if total is None else total + product
        if last:
            out[f // 2, :, (f % 2) * 64 : (f % 2 + 1) * 64] = total.astype(out.dtype)
        else:
            out[f] = total


def apply_tables(planes, tables, start, before, kind):
    n_bins = tables[0].shape[1]
    shape = (n_bins, 128, 64) if kind is None else (n_bins // 2, 128, 128)
    args = (*planes, *tables) + (() if before is None else (before,))
    return pl.pallas_call(
        lambda *refs: apply_kernel(
            len(planes), len(tables), start, before is not None, kind is not None, *refs
        ),
        in_specs=[VMEM] * len(args),
        out_specs=VMEM,
        out_shape=pltpu.VMEM(shape, kind or jnp.float32),
        compiler_params=PARAMS,
        name="apply",
    )(*args)


def power_kernel(scale, mine, theirs, out):
    for k in range(mine.shape[0]):
        total = mine[k] + theirs[k].astype(jnp.float32)
        squares = (total * total).T
        for f in range(2):
            power = jnp.sum(squares[f * 64 : (f + 1) * 64], axis=0, keepdims=True)
            out[2 * k + f : 2 * k + f + 1, :] = power * scale


def powers(mine, theirs, scale):
    return pl.pallas_call(
        lambda *refs: power_kernel(scale, *refs),
        in_specs=[VMEM] * 2,
        out_specs=VMEM,
        out_shape=jax.ShapeDtypeStruct((2 * mine.shape[0], mine.shape[1]), jnp.float32),
        compiler_params=PARAMS,
        name="powers",
    )(mine, theirs)


def route(move):
    pairs = []
    for tm in range(4):
        for mic in range(32):
            zh, core, y, x, zl = tm // 2, tm % 2, mic // 8, mic // 2 % 4, mic % 2
            zh, core, y, x, zl = move(zh, core, y, x, zl)
            pairs.append((tm * 32 + mic, (zh * 2 + core) * 32 + y % 4 * 8 + x % 4 * 2 + zl))
    return pairs


def send(value, move):
    return lax.ppermute(value, AXES, route(move))


def per_device(samples, bin_ids, delays):
    keep, give, own_delays, half = transform(bin_ids, delays, samples)
    got = send(give, lambda zh, c, y, x, zl: (zh, 1 - c, y, x, zl))
    half = send(half, lambda zh, c, y, x, zl: (zh, c, y, x, 1 - zl))
    partner_delays = (half,)
    away = jnp.concatenate([keep[1:], got[1:]])
    far = send(away, lambda zh, c, y, x, zl: (1 - zh, c, y, x, zl))
    column = jnp.concatenate([keep[:1], got[:1], far])

    own, start = [], 0
    for pairs in OWN:
        own.append(steer_tables(bin_ids, (own_delays,), start, pairs))
        start += pairs
    partner = steer_tables(bin_ids, partner_delays, 0, 8)

    def first(d):
        return lambda zh, c, y, x, zl: (zh, c, y + d, x, zl) if c else (zh, c, y, x + d, zl)

    def second(d):
        return lambda zh, c, y, x, zl: (zh, c, y, x + d, zl) if c else (zh, c, y + d, x, zl)

    line = [column]
    for d in SHIFTS:
        line.append(send(column, first(d)))
    line = jnp.stack(line)
    planes = [line]
    for d in SHIFTS:
        planes.append(send(line, second(d)))
    theirs = apply_tables(planes[:1], (partner,), 0, None, None)
    theirs = apply_tables(planes[2:], (partner,), 4, theirs, None)
    theirs = apply_tables(planes[1:2], (partner,), 2, theirs, jnp.bfloat16)
    theirs = send(theirs, lambda zh, c, y, x, zl: (zh, c, y, x, 1 - zl))
    mine = apply_tables(planes, own, 0, None, jnp.float32)
    seg_count = samples.shape[0] * lax.axis_size("tm")
    return powers(mine, theirs, 1.0 / (delays.shape[1] * seg_count))


def solution(mesh):
    placed = (P("tm", "mic", None), P(), P("mic", None))
    return jax.shard_map(
        per_device, mesh=mesh, in_specs=placed, out_specs=P("tm", "mic"), check_vma=False
    )
```

```python
import math

import jax
import jax.numpy as jnp
from jax import lax
from jax.experimental import pallas as pl
from jax.experimental.pallas import tpu as pltpu
from jax.sharding import PartitionSpec as P


AXES = ("tm", "mic")
SHIFTS = (2, 1, 3)
ROUND = 12582912.0
GROUPS = (2, 3, 3)
AHEAD = 4
OWN = (2, 4, 2)
SIN_POLY = (4.442882919124343, -7.30824568650904, 3.6063542184324877, -0.8461116503718901, 0.10982451642219883)
COS_POLY = (1.414213496255228, -6.978850948563807, 5.73946037690717, -1.8835579059870113, 0.31068802752761115)


def horner(coefs, z):
    value = coefs[-1]
    for coef in coefs[-2::-1]:
        value = value * z + coef
    return value


def cos_sin(turns):
    r = turns - ((turns + ROUND) - ROUND)
    z = r * r
    s = horner(SIN_POLY, z) * r
    c = horner(COS_POLY, z)
    return 1.0 - s * s, s * c


VMEM = pl.BlockSpec(memory_space=pltpu.VMEM)
SMEM = pl.BlockSpec(memory_space=pltpu.SMEM)
PARAMS = pltpu.CompilerParams(vmem_limit_bytes=16 * 2**20)
WIDE = pltpu.CompilerParams(vmem_limit_bytes=58 * 2**20)


def position():
    tm = lax.axis_index("tm")
    mic = lax.axis_index("mic")
    return tm >> 1, tm & 1, mic >> 3, (mic >> 1) & 3, mic & 1


def transform_kernel(
    bins_in, delays_in, samples, keep, send, mine, half, bins, delays, segs, sems, table, sums, blocks
):
    zh, core, _, _, zl = position()
    n_segs, mics, length = segs.shape
    n_bins = bins.shape[0]
    chunk = 512
    copies = [
        pltpu.make_async_copy(samples.at[s], segs.at[s], sems.at[s]) for s in range(n_segs)
    ]
    bins_copy = pltpu.make_async_copy(bins_in, bins, sems.at[n_segs])
    delays_copy = pltpu.make_async_copy(delays_in, delays, sems.at[n_segs + 1])
    bins_copy.start()
    for s in range(AHEAD):
        copies[s].start()

    bins_copy.wait()
    row = lax.broadcasted_iota(jnp.int32, (n_bins, chunk), 0)
    scale = jnp.zeros((n_bins, chunk), jnp.float32)
    for b in range(n_bins):
        scale = jnp.where(row == b, bins[b].astype(jnp.float32) * (1.0 / length), scale)
    lane = lax.broadcasted_iota(jnp.int32, (n_bins, chunk), 1)
    for k in range(length // chunk):
        n = (lane + k * chunk).astype(jnp.float32)
        hann = 0.5 - 0.5 * cos_sin(n[0:8] * (1.0 / length))[0]
        weight = jnp.concatenate([hann, hann], axis=0) * (1.0 / math.sqrt(0.375 * length))
        cos, sin = cos_sin(n * scale)
        table[0:n_bins, k * chunk : (k + 1) * chunk] = (weight * cos).astype(jnp.bfloat16)
        table[n_bins:, k * chunk : (k + 1) * chunk] = (-weight * sin).astype(jnp.bfloat16)

    done = 0
    for g, group in enumerate(GROUPS):
        for s in range(done, done + group):
            copies[s].wait()
            if s + AHEAD < n_segs:
                copies[s + AHEAD].start()
        if g == 0:
            delays_copy.start()
        if g == len(GROUPS) - 1:
            delays_copy.wait()
        product = lax.dot_general(
            segs[done : done + group].reshape(group * mics, length),
            table[...],
            (((1,), (1,)), ((), ())),
            preferred_element_type=jnp.float32,
        )
        for s in range(group):
            sums[done + s] = product[s * mics : (s + 1) * mics].T
        done += group

    for j in range(mine.shape[0]):
        first = delays[:, j * 256 : j * 256 + 128]
        second = delays[:, j * 256 + 128 : (j + 1) * 256]
        mine[j] = jnp.where(zl == 0, first, second).astype(jnp.int16)
        other = jnp.where(zl == 0, second, first).astype(jnp.int16)

        half[j] = other

    for b in range(n_bins):
        rows = jnp.concatenate([sums[:, b, :], sums[:, n_bins + b, :]], axis=0)
        blocks[b // 4, (b % 4) * 16 : (b % 4 + 1) * 16, :] = rows.astype(jnp.bfloat16)
    keep[0] = blocks[zh * 2 + core]
    keep[1] = blocks[(1 - zh) * 2 + core]
    send[0] = blocks[zh * 2 + 1 - core]
    send[1] = blocks[(1 - zh) * 2 + 1 - core]


def transform(bins, delays, samples):
    segs, mics, length = samples.shape
    points = delays.shape[0]
    n_bins = bins.shape[0]
    block = (2, n_bins // 4 * 2 * segs, mics)
    blocks = delays.shape[1] // 256
    return pl.pallas_call(
        transform_kernel,
        in_specs=[pl.BlockSpec(memory_space=pltpu.HBM)] * 3,
        out_specs=[VMEM] * 4,
        out_shape=[
            pltpu.VMEM(block, jnp.bfloat16),
            pltpu.VMEM(block, jnp.bfloat16),
            pltpu.VMEM((blocks, points, 128), jnp.int16),
            pltpu.VMEM((blocks, points, 128), jnp.int16),
        ],
        scratch_shapes=[
            pltpu.SMEM((n_bins,), jnp.int32),
            pltpu.VMEM(delays.shape, delays.dtype),
            pltpu.VMEM((segs, mics, length), jnp.bfloat16),
            pltpu.SemaphoreType.DMA((segs + 2,)),
            pltpu.VMEM((2 * n_bins, length), jnp.bfloat16),
            pltpu.VMEM((segs, 2 * n_bins, mics), jnp.float32),
            pltpu.VMEM((4,) + block[1:], jnp.bfloat16),
        ],
        compiler_params=WIDE,
        name="transform",
    )(bins, delays, samples)


def arrival(index):
    return ((index & 1) << 1) | (index >> 1)


def block_of(index):
    _, core, y, x, _ = position()
    second = arrival(index >> 2)
    first = arrival(index & 3)
    dx = first + core * (second - first)
    dy = second + core * (first - second)
    return ((y - dy) & 3) * 4 + ((x - dx) & 3)


def steer_kernel(start, halves, bins, *refs):
    out = refs[-1]
    pairs, n_bins, points, _ = out.shape
    tm = lax.axis_index("tm")
    core = tm & 1
    turns = [bins[tm * n_bins + f].astype(jnp.float32) * (1.0 / 4096) for f in range(n_bins)]

    def body(pair, carry):
        for half in range(2):
            block = block_of((start + pair) * 2 + half)
            for k in range(points // 32):
                rows = slice(k * 32, (k + 1) * 32)
                if halves:
                    kept = (block >> 3) == core
                    d = jnp.where(kept, refs[0][block & 7, rows, :], refs[1][block & 7, rows, :])
                else:
                    d = refs[0][block, rows, :]
                d = d.astype(jnp.int32).astype(jnp.float32)
                for f in range(n_bins):
                    cos, sin = cos_sin(d * turns[f])
                    out[pair, f, rows, half * 128 : (half + 1) * 128] = cos.astype(jnp.bfloat16)
                    out[pair, f, rows, 256 + half * 128 : 384 + half * 128] = sin.astype(jnp.bfloat16)
        return carry

    lax.fori_loop(0, pairs, body, 0)


def steer_tables(bins, delays, start, pairs):
    return pl.pallas_call(
        lambda *refs: steer_kernel(start, len(delays) == 2, *refs),
        in_specs=[SMEM] + [VMEM] * len(delays),
        out_specs=VMEM,
        out_shape=pltpu.VMEM((pairs, bins.shape[0] // 4, 128, 512), jnp.bfloat16),
        compiler_params=PARAMS,
        name="steer",
    )(bins, *delays)


def apply_kernel(n_planes, n_tables, start, carried, last, *refs):
    planes = refs[:n_planes]
    tables = refs[n_planes : n_planes + n_tables]
    before = refs[n_planes + n_tables] if carried else None
    out = refs[-1]
    pairs = [(table, p) for table in tables for p in range(table.shape[0])]
    n_bins = tables[0].shape[1]
    for f in range(n_bins):
        total = before[f] if carried else None
        for i, plane in enumerate(planes):
            for q in range(2):
                cos_cols, sin_cols = [], []
                for h in range(2):
                    both = [
                        plane[2 * q + h, src, f * 16 : (f + 1) * 16, :].astype(jnp.float32)
                        for src in range(4)
                    ]
                    real = [b[0:8] for b in both]
                    imag = [b[8:16] for b in both]
                    cos_cols.append(jnp.concatenate(real + imag, axis=0))
                    sin_cols.append(jnp.concatenate([-v for v in imag] + real, axis=0))
                columns = jnp.concatenate(cos_cols + sin_cols, axis=1).astype(jnp.bfloat16)
                table, p = pairs[start + 2 * i + q]
                product = lax.dot_general(
                    table[p, f],
                    columns,
                    (((1,), (1,)), ((), ())),
                    preferred_element_type=jnp.float32,
                )
                total = product if total is None else total + product
        if last:
            out[f // 2, :, (f % 2) * 64 : (f % 2 + 1) * 64] = total.astype(out.dtype)
        else:
            out[f] = total


def apply_tables(planes, tables, start, before, kind):
    n_bins = tables[0].shape[1]
    shape = (n_bins, 128, 64) if kind is None else (n_bins // 2, 128, 128)
    args = (*planes, *tables) + (() if before is None else (before,))
    return pl.pallas_call(
        lambda *refs: apply_kernel(
            len(planes), len(tables), start, before is not None, kind is not None, *refs
        ),
        in_specs=[VMEM] * len(args),
        out_specs=VMEM,
        out_shape=pltpu.VMEM(shape, kind or jnp.float32),
        compiler_params=PARAMS,
        name="apply",
    )(*args)


def power_kernel(scale, mine, theirs, out):
    for k in range(mine.shape[0]):
        total = mine[k] + theirs[k].astype(jnp.float32)
        squares = (total * total).T
        for f in range(2):
            power = jnp.sum(squares[f * 64 : (f + 1) * 64], axis=0, keepdims=True)
            out[2 * k + f : 2 * k + f + 1, :] = power * scale


def powers(mine, theirs, scale):
    return pl.pallas_call(
        lambda *refs: power_kernel(scale, *refs),
        in_specs=[VMEM] * 2,
        out_specs=VMEM,
        out_shape=jax.ShapeDtypeStruct((2 * mine.shape[0], mine.shape[1]), jnp.float32),
        compiler_params=PARAMS,
        name="powers",
    )(mine, theirs)


def route(move):
    pairs = []
    for tm in range(4):
        for mic in range(32):
            zh, core, y, x, zl = tm // 2, tm % 2, mic // 8, mic // 2 % 4, mic % 2
            zh, core, y, x, zl = move(zh, core, y, x, zl)
            pairs.append((tm * 32 + mic, (zh * 2 + core) * 32 + y % 4 * 8 + x % 4 * 2 + zl))
    return pairs


def send(value, move):
    return lax.ppermute(value, AXES, route(move))


def per_device(samples, bin_ids, delays):
    keep, give, own_delays, half = transform(bin_ids, delays, samples)
    got = send(give, lambda zh, c, y, x, zl: (zh, 1 - c, y, x, zl))
    half = send(half, lambda zh, c, y, x, zl: (zh, c, y, x, 1 - zl))
    partner_delays = (half,)
    away = jnp.concatenate([keep[1:], got[1:]])
    far = send(away, lambda zh, c, y, x, zl: (1 - zh, c, y, x, zl))
    column = jnp.concatenate([keep[:1], got[:1], far])

    own, start = [], 0
    for pairs in OWN:
        own.append(steer_tables(bin_ids, (own_delays,), start, pairs))
        start += pairs
    partner = steer_tables(bin_ids, partner_delays, 0, 8)

    def first(d):
        return lambda zh, c, y, x, zl: (zh, c, y + d, x, zl) if c else (zh, c, y, x + d, zl)

    def second(d):
        return lambda zh, c, y, x, zl: (zh, c, y, x + d, zl) if c else (zh, c, y + d, x, zl)

    line = [column]
    for d in SHIFTS:
        line.append(send(column, first(d)))
    line = jnp.stack(line)
    planes = [line]
    for d in SHIFTS:
        planes.append(send(line, second(d)))
    theirs = apply_tables(planes[:1], (partner,), 0, None, None)
    theirs = apply_tables(planes[2:], (partner,), 4, theirs, None)
    theirs = apply_tables(planes[1:2], (partner,), 2, theirs, jnp.bfloat16)
    theirs = send(theirs, lambda zh, c, y, x, zl: (zh, c, y, x, 1 - zl))
    mine = apply_tables(planes, own, 0, None, jnp.float32)
    seg_count = samples.shape[0] * lax.axis_size("tm")
    return powers(mine, theirs, 1.0 / (delays.shape[1] * seg_count))


def solution(mesh):
    placed = (P("tm", "mic", None), P(), P("mic", None))
    return jax.shard_map(
        per_device, mesh=mesh, in_specs=placed, out_specs=P("tm", "mic"), check_vma=False
    )
```

```python
import math

import jax
import jax.numpy as jnp
from jax import lax
from jax.experimental import pallas as pl
from jax.experimental.pallas import tpu as pltpu
from jax.sharding import PartitionSpec as P


AXES = ("tm", "mic")
SHIFTS = (2, 1, 3)
ROUND = 12582912.0
GROUPS = (2, 3, 3)
AHEAD = 4
OWN = (2, 4, 2)
SIN_POLY = (4.442882919124343, -7.30824568650904, 3.6063542184324877, -0.8461116503718901, 0.10982451642219883)
COS_POLY = (1.414213496255228, -6.978850948563807, 5.73946037690717, -1.8835579059870113, 0.31068802752761115)


def horner(coefs, z):
    value = coefs[-1]
    for coef in coefs[-2::-1]:
        value = value * z + coef
    return value


def cos_sin(turns):
    r = turns - ((turns + ROUND) - ROUND)
    z = r * r
    s = horner(SIN_POLY, z) * r
    c = horner(COS_POLY, z)
    return 1.0 - s * s, s * c


VMEM = pl.BlockSpec(memory_space=pltpu.VMEM)
SMEM = pl.BlockSpec(memory_space=pltpu.SMEM)
PARAMS = pltpu.CompilerParams(vmem_limit_bytes=16 * 2**20)
WIDE = pltpu.CompilerParams(vmem_limit_bytes=58 * 2**20)


def position():
    tm = lax.axis_index("tm")
    mic = lax.axis_index("mic")
    return tm >> 1, tm & 1, mic >> 3, (mic >> 1) & 3, mic & 1


def transform_kernel(
    bins_in, delays_in, samples, keep, send, mine, half, bins, delays, segs, sems, table, sums, blocks
):
    zh, core, _, _, zl = position()
    n_segs, mics, length = segs.shape
    n_bins = bins.shape[0]
    chunk = 512
    copies = [
        pltpu.make_async_copy(samples.at[s], segs.at[s], sems.at[s]) for s in range(n_segs)
    ]
    bins_copy = pltpu.make_async_copy(bins_in, bins, sems.at[n_segs])
    delays_copy = pltpu.make_async_copy(delays_in, delays, sems.at[n_segs + 1])
    bins_copy.start()
    for s in range(AHEAD):
        copies[s].start()

    bins_copy.wait()
    row = lax.broadcasted_iota(jnp.int32, (n_bins, chunk), 0)
    scale = jnp.zeros((n_bins, chunk), jnp.float32)
    for b in range(n_bins):
        scale = jnp.where(row == b, bins[b].astype(jnp.float32) * (1.0 / length), scale)
    lane = lax.broadcasted_iota(jnp.int32, (n_bins, chunk), 1)
    for k in range(length // chunk):
        n = (lane + k * chunk).astype(jnp.float32)
        hann = 0.5 - 0.5 * cos_sin(n[0:8] * (1.0 / length))[0]
        weight = jnp.concatenate([hann, hann], axis=0) * (1.0 / math.sqrt(0.375 * length))
        cos, sin = cos_sin(n * scale)
        table[0:n_bins, k * chunk : (k + 1) * chunk] = (weight * cos).astype(jnp.bfloat16)
        table[n_bins:, k * chunk : (k + 1) * chunk] = (-weight * sin).astype(jnp.bfloat16)

    done = 0
    for g, group in enumerate(GROUPS):
        for s in range(done, done + group):
            copies[s].wait()
            if s + AHEAD < n_segs:
                copies[s + AHEAD].start()
        if g == 0:
            delays_copy.start()
        if g == len(GROUPS) - 1:
            delays_copy.wait()
        product = lax.dot_general(
            segs[done : done + group].reshape(group * mics, length),
            table[...],
            (((1,), (1,)), ((), ())),
            preferred_element_type=jnp.float32,
        )
        for s in range(group):
            sums[done + s] = product[s * mics : (s + 1) * mics].T
        done += group

    for j in range(mine.shape[0]):
        first = delays[:, j * 256 : j * 256 + 128]
        second = delays[:, j * 256 + 128 : (j + 1) * 256]
        mine[j] = jnp.where(zl == 0, first, second).astype(jnp.int16)
        other = jnp.where(zl == 0, second, first).astype(jnp.int16)

        half[j] = other

    for b in range(n_bins):
        rows = jnp.concatenate([sums[:, b, :], sums[:, n_bins + b, :]], axis=0)
        blocks[b // 4, (b % 4) * 16 : (b % 4 + 1) * 16, :] = rows.astype(jnp.bfloat16)
    keep[0] = blocks[zh * 2 + core]
    keep[1] = blocks[(1 - zh) * 2 + core]
    send[0] = blocks[zh * 2 + 1 - core]
    send[1] = blocks[(1 - zh) * 2 + 1 - core]


def transform(bins, delays, samples):
    segs, mics, length = samples.shape
    points = delays.shape[0]
    n_bins = bins.shape[0]
    block = (2, n_bins // 4 * 2 * segs, mics)
    blocks = delays.shape[1] // 256
    return pl.pallas_call(
        transform_kernel,
        in_specs=[pl.BlockSpec(memory_space=pltpu.HBM)] * 3,
        out_specs=[VMEM] * 4,
        out_shape=[
            pltpu.VMEM(block, jnp.bfloat16),
            pltpu.VMEM(block, jnp.bfloat16),
            pltpu.VMEM((blocks, points, 128), jnp.int16),
            pltpu.VMEM((blocks, points, 128), jnp.int16),
        ],
        scratch_shapes=[
            pltpu.SMEM((n_bins,), jnp.int32),
            pltpu.VMEM(delays.shape, delays.dtype),
            pltpu.VMEM((segs, mics, length), jnp.bfloat16),
            pltpu.SemaphoreType.DMA((segs + 2,)),
            pltpu.VMEM((2 * n_bins, length), jnp.bfloat16),
            pltpu.VMEM((segs, 2 * n_bins, mics), jnp.float32),
            pltpu.VMEM((4,) + block[1:], jnp.bfloat16),
        ],
        compiler_params=WIDE,
        name="transform",
    )(bins, delays, samples)


def arrival(index):
    return ((index & 1) << 1) | (index >> 1)


def block_of(index):
    _, core, y, x, _ = position()
    second = arrival(index >> 2)
    first = arrival(index & 3)
    dx = first + core * (second - first)
    dy = second + core * (first - second)
    return ((y - dy) & 3) * 4 + ((x - dx) & 3)


def steer_kernel(start, halves, bins, *refs):
    out = refs[-1]
    pairs, n_bins, points, _ = out.shape
    tm = lax.axis_index("tm")
    core = tm & 1
    turns = [bins[tm * n_bins + f].astype(jnp.float32) * (1.0 / 4096) for f in range(n_bins)]

    def body(pair, carry):
        for half in range(2):
            block = block_of((start + pair) * 2 + half)
            for k in range(points // 32):
                rows = slice(k * 32, (k + 1) * 32)
                if halves:
                    kept = (block >> 3) == core
                    d = jnp.where(kept, refs[0][block & 7, rows, :], refs[1][block & 7, rows, :])
                else:
                    d = refs[0][block, rows, :]
                d = d.astype(jnp.int32).astype(jnp.float32)
                for f in range(n_bins):
                    cos, sin = cos_sin(d * turns[f])
                    out[pair, f, rows, half * 128 : (half + 1) * 128] = cos.astype(jnp.bfloat16)
                    out[pair, f, rows, 256 + half * 128 : 384 + half * 128] = sin.astype(jnp.bfloat16)
        return carry

    lax.fori_loop(0, pairs, body, 0)


def steer_tables(bins, delays, start, pairs):
    return pl.pallas_call(
        lambda *refs: steer_kernel(start, len(delays) == 2, *refs),
        in_specs=[SMEM] + [VMEM] * len(delays),
        out_specs=VMEM,
        out_shape=pltpu.VMEM((pairs, bins.shape[0] // 4, 128, 512), jnp.bfloat16),
        compiler_params=PARAMS,
        name="steer",
    )(bins, *delays)


def apply_kernel(n_planes, n_tables, start, carried, last, *refs):
    planes = refs[:n_planes]
    tables = refs[n_planes : n_planes + n_tables]
    before = refs[n_planes + n_tables] if carried else None
    out = refs[-1]
    pairs = [(table, p) for table in tables for p in range(table.shape[0])]
    n_bins = tables[0].shape[1]
    for f in range(n_bins):
        total = before[f] if carried else None
        for i, plane in enumerate(planes):
            for q in range(2):
                cos_cols, sin_cols = [], []
                for h in range(2):
                    both = [
                        plane[2 * q + h, src, f * 16 : (f + 1) * 16, :].astype(jnp.float32)
                        for src in range(4)
                    ]
                    real = [b[0:8] for b in both]
                    imag = [b[8:16] for b in both]
                    cos_cols.append(jnp.concatenate(real + imag, axis=0))
                    sin_cols.append(jnp.concatenate([-v for v in imag] + real, axis=0))
                columns = jnp.concatenate(cos_cols + sin_cols, axis=1).astype(jnp.bfloat16)
                table, p = pairs[2 * start[i] + q]
                product = lax.dot_general(
                    table[p, f],
                    columns,
                    (((1,), (1,)), ((), ())),
                    preferred_element_type=jnp.float32,
                )
                total = product if total is None else total + product
        if last:
            out[f // 2, :, (f % 2) * 64 : (f % 2 + 1) * 64] = total.astype(out.dtype)
        else:
            out[f] = total


def apply_tables(planes, tables, start, before, kind):
    n_bins = tables[0].shape[1]
    shape = (n_bins, 128, 64) if kind is None else (n_bins // 2, 128, 128)
    args = (*planes, *tables) + (() if before is None else (before,))
    return pl.pallas_call(
        lambda *refs: apply_kernel(
            len(planes), len(tables), start, before is not None, kind is not None, *refs
        ),
        in_specs=[VMEM] * len(args),
        out_specs=VMEM,
        out_shape=pltpu.VMEM(shape, kind or jnp.float32),
        compiler_params=PARAMS,
        name="apply",
    )(*args)


def power_kernel(scale, mine, theirs, out):
    for k in range(mine.shape[0]):
        total = mine[k] + theirs[k].astype(jnp.float32)
        squares = (total * total).T
        for f in range(2):
            power = jnp.sum(squares[f * 64 : (f + 1) * 64], axis=0, keepdims=True)
            out[2 * k + f : 2 * k + f + 1, :] = power * scale


def powers(mine, theirs, scale):
    return pl.pallas_call(
        lambda *refs: power_kernel(scale, *refs),
        in_specs=[VMEM] * 2,
        out_specs=VMEM,
        out_shape=jax.ShapeDtypeStruct((2 * mine.shape[0], mine.shape[1]), jnp.float32),
        compiler_params=PARAMS,
        name="powers",
    )(mine, theirs)


def route(move):
    pairs = []
    for tm in range(4):
        for mic in range(32):
            zh, core, y, x, zl = tm // 2, tm % 2, mic // 8, mic // 2 % 4, mic % 2
            zh, core, y, x, zl = move(zh, core, y, x, zl)
            pairs.append((tm * 32 + mic, (zh * 2 + core) * 32 + y % 4 * 8 + x % 4 * 2 + zl))
    return pairs


def send(value, move):
    return lax.ppermute(value, AXES, route(move))


def per_device(samples, bin_ids, delays):
    keep, give, own_delays, half = transform(bin_ids, delays, samples)
    got = send(give, lambda zh, c, y, x, zl: (zh, 1 - c, y, x, zl))
    half = send(half, lambda zh, c, y, x, zl: (zh, c, y, x, 1 - zl))
    partner_delays = (half,)
    away = jnp.concatenate([keep[1:], got[1:]])
    far = send(away, lambda zh, c, y, x, zl: (1 - zh, c, y, x, zl))
    column = jnp.concatenate([keep[:1], got[:1], far])

    own, start = [], 0
    for pairs in OWN:
        own.append(steer_tables(bin_ids, (own_delays,), start, pairs))
        start += pairs
    partner = steer_tables(bin_ids, partner_delays, 0, 8)

    def first(d):
        return lambda zh, c, y, x, zl: (zh, c, y + d, x, zl) if c else (zh, c, y, x + d, zl)

    def second(d):
        return lambda zh, c, y, x, zl: (zh, c, y, x + d, zl) if c else (zh, c, y + d, x, zl)

    line = [column]
    for d in SHIFTS:
        line.append(send(column, first(d)))
    line = jnp.stack(line)
    planes = [line]
    for d in SHIFTS:
        planes.append(send(line, second(d)))
    early = (planes[0], planes[2], planes[3])
    theirs = apply_tables(early, (partner,), (0, 2, 3), None, None)
    theirs = apply_tables(planes[1:2], (partner,), (1,), theirs, jnp.bfloat16)
    theirs = send(theirs, lambda zh, c, y, x, zl: (zh, c, y, x, 1 - zl))
    mine = apply_tables(planes, own, (0, 1, 2, 3), None, jnp.float32)
    seg_count = samples.shape[0] * lax.axis_size("tm")
    return powers(mine, theirs, 1.0 / (delays.shape[1] * seg_count))


def solution(mesh):
    placed = (P("tm", "mic", None), P(), P("mic", None))
    return jax.shard_map(
        per_device, mesh=mesh, in_specs=placed, out_specs=P("tm", "mic"), check_vma=False
    )
```
